256 devices in a mesh: replica: 16 (over z_lo, x), fsdp: 16 (over y, z_hi, core).
Axes of the slice: x: 4, y: 4, z: 8 (z_hi: 2, z_lo: 4; z = z_hi * 4 + z_lo), core: 2. Of those that a mesh axis runs over, the one named last changes fastest.
Arguments:
- base: float32 [8192, 1024], P('fsdp'), may hold values from -6 to 6
- local: bfloat16 [16, 8192, 1024], P('replica', 'fsdp'), may hold values from -6 to 6
- momentum: float32 [8192, 1024], P('fsdp'), may hold values from -6 to 6
- tokens: bfloat16 [16, 2048, 8192], P('replica', 'fsdp'), may hold values from -6 to 6
- mask_embed: bfloat16 [8192], replicated, may hold values from -6 to 6
- mask_pos: int32 [16, 1, 768], P('replica'), may hold values from 0 to 2047, as said below
- cotangent: bfloat16 [16, 2048, 1024], P('replica', 'fsdp'), may hold values from -6 to 6
Outputs:
- new_momentum: bfloat16 [8192, 1024], P('fsdp')
- stepped: bfloat16 [16, 8192, 1024], P('replica', 'fsdp')
The draws below stay inside these ranges and needn't reach their ends.
Inputs may be any that keep to these rules, and one draw needn't show every extreme that they name: `mask_pos`: each row holds 768 different positions of its sequence.
All inputs are finite; a program needn't handle non-finite values. Where the reference program divides by a largest or mean magnitude, that divisor is 1e-20 or more.
Results may differ from the reference program's by a relative error of at most 0.008.
Values may be sent and summed in bfloat16 or wider, within the bound.
A program may use at most 128 MiB of HBM per device.

```python
import jax
import jax.numpy as jnp
from jax import lax

D = 8192
KVW = 1024
QBLOCK = 128
LENGTH = 2048
NMASK = 768
SEQS = 1
TOKENS_R = 2048
N_REPLICA = 16
N_FSDP = 16


def draw_mask_pos(key, part):
    scores = jax.random.randint(key, (N_REPLICA, SEQS, LENGTH), 0, LENGTH, dtype=jnp.int32)
    scores = scores * LENGTH + jnp.arange(LENGTH, dtype=jnp.int32)[None, None, :]
    order = jnp.argsort(scores, axis=-1, stable=True)
    return order[:, :, :NMASK].astype(jnp.int32)


def block_scale(own_key, extent, split, least, top_value):
    def one(dim, parts):
        draws = jax.random.uniform(jax.random.fold_in(jax.random.fold_in(own_key, 6), dim), (parts,), jnp.float32, least / len(split), top_value / len(split))
        return jnp.repeat(jnp.exp(draws), extent[dim] // parts).reshape((-1,) + (1,) * (len(extent) - dim - 1))

    factor_of = one(*split[0])
    for cut in split[1:]:
        factor_of = factor_of * one(*cut)
    return factor_of


def normal_values(key, extent, spread, reach, cuts=(), held_as=jnp.bfloat16):
    factor_of = block_scale(key, extent, cuts, -0.22, 0.18) if cuts else 1.0
    entries = jax.random.normal(key, extent, jnp.float32) * spread * factor_of
    return jnp.minimum(jnp.maximum(entries, -reach), reach).astype(held_as)


def setup_inputs(seed: int = 0) -> dict:
    keys = jax.random.split(jax.random.key(seed), 8)
    return {
        "base": normal_values(keys[0], (D, KVW), 1.0, 6.0, ((0, 16),), jnp.float32),
        "local": normal_values(keys[1], (N_REPLICA, D, KVW), 1.0, 6.0, ((0, 16), (1, 16))),
        "momentum": normal_values(keys[2], (D, KVW), 1.0, 6.0, ((0, 16),), jnp.float32),
        "tokens": normal_values(keys[3], (N_REPLICA, TOKENS_R, D), 1.0, 6.0, ((0, 16), (1, 16))),
        "mask_embed": normal_values(keys[4], (D,), 1.0, 6.0),
        "mask_pos": draw_mask_pos(jax.random.fold_in(keys[7], 71), 0),
        "cotangent": normal_values(keys[6], (N_REPLICA, TOKENS_R, KVW), 1.0, 6.0, ((0, 16), (1, 16))),
    }


momentum_decay = 0.9
outer_rate = 0.7
inner_rate = 0.5


def dequantize(base, replica_params):
    drift = base - replica_params.astype(jnp.float32)
    blocks = drift.reshape(D, KVW // QBLOCK, QBLOCK)
    scales = (jnp.max(jnp.abs(blocks), axis=2, keepdims=True) + 1e-6).astype(jnp.bfloat16)
    code_vals = (blocks / scales.astype(jnp.float32)).astype(jnp.bfloat16)
    return (code_vals.astype(jnp.float32) * scales.astype(jnp.float32)).reshape(D, KVW)


def reference(base, local, momentum, tokens, mask_embed, mask_pos, cotangent):
    def add_replica(total, replica_params):
        return total + dequantize(base, replica_params), None

    summed, _ = lax.scan(add_replica, jnp.zeros((D, KVW), jnp.float32), local)
    outer_grad = summed / N_REPLICA
    momentum_next = momentum_decay * momentum + outer_grad
    renewed = base - outer_rate * (outer_grad + momentum_decay * momentum_next)

    def inner_step(triple):
        tok_block, positions, upstream = triple
        seq_index = jnp.arange(SEQS, dtype=jnp.int32)[:, None]
        marks = jnp.zeros((SEQS, LENGTH), jnp.int32).at[seq_index, positions].set(1).reshape(-1)
        inputs = jnp.where(marks[:, None] > 0, mask_embed[None, :], tok_block)
        group_in = inputs.reshape(N_FSDP, -1, D)
        group_up = upstream.reshape(N_FSDP, -1, KVW)

        def add_group(total, pair):
            term = lax.dot_general(pair[0], pair[1], (((0,), (0,)), ((), ())), preferred_element_type=jnp.float32)
            rounded = lax.optimization_barrier(term.astype(jnp.bfloat16))
            return total + rounded.astype(jnp.float32), None

        grad_sum, _ = lax.scan(add_group, jnp.zeros((D, KVW), jnp.float32), (group_in, group_up))
        gradient = grad_sum * (D ** -0.5)
        return (renewed - inner_rate * gradient).astype(jnp.bfloat16)

    stepped = lax.map(inner_step, (tokens, mask_pos, cotangent))
    return momentum_next.astype(jnp.bfloat16), stepped
```

```python
import jax
import jax.numpy as jnp
from jax import lax
from jax.experimental import pallas as pl
from jax.experimental.pallas import tpu as pltpu
from jax.sharding import PartitionSpec as P

D = 8192
ROWS = 512
COLS = 1024
TOK = 128
QBLOCK = 128
NB = 4
CB = COLS // NB
NA = 4
CA = ROWS // NA
HALF = 1024

momentum_decay = 0.9
outer_rate = 0.7
inner_rate = 0.5

MESH = pl.DeviceIdType.MESH
BF = jnp.bfloat16
F32 = jnp.float32


def al(v, m):
    return pl.multiple_of(v, m)


def kernel(base_h, local_h, mom_h, tok_h, emb_ref, pos_ref, cot_h, nm_h, st_h,
           base_v, mom_v, lr, r2s, r2r, own, og, xa, xo, cb, mask_v, ev, ps, pr, q, nm_v, st_v,
           s_c, s_f, s_a, s_o, s_p, s_r1, s_r2, s_r3, s_r4,
           v_c, v_f, v_a, v_o, v_p, v_r1, v_r2, v_r3, v_r4, l_sem):
    r = lax.axis_index("replica")
    f = lax.axis_index("fsdp")
    zl, x = lax.div(r, 4), lax.rem(r, 4)
    y, h, c = lax.div(f, 4), lax.rem(lax.div(f, 2), 2), lax.rem(f, 2)
    slot = c * 4 + y

    def dev(zl_, x_, y_, h_, c_):
        return {"replica": zl_ * 4 + x_, "fsdp": y_ * 4 + h_ * 2 + c_}

    def half(k):
        t = lax.rem(slot + k, 8)
        return lax.rem(t, 4), lax.div(t, 4)

    def to_y(k):
        return dev(zl, x, lax.rem(y + k, 4), h, c)

    def to_x(k):
        return dev(zl, lax.rem(x + k, 4), y, h, c)

    def to_z(k):
        return dev(lax.rem(zl + k, 4), x, y, h, c)

    other_core = dev(zl, x, y, h, 1 - c)
    antipode = dev(zl, x, y, 1 - h, c)

    def send(src, dst, ss, rs, to):
        cp = pltpu.make_async_remote_copy(
            src_ref=src, dst_ref=dst, send_sem=ss, recv_sem=rs, device_id=to, device_id_type=MESH
        )
        cp.start()
        return cp

    def await_bytes(ref, sem):
        pltpu.make_async_copy(ref, ref, sem).wait()

    load_base = pltpu.make_async_copy(base_h, base_v, l_sem.at[0])
    load_mom = pltpu.make_async_copy(mom_h, mom_v, l_sem.at[1])
    load_base.start()
    load_mom.start()

    barrier = pltpu.get_barrier_semaphore()
    partners = [other_core, antipode]
    for k in (1, 2, 3):
        partners += [to_x(k), to_z(k)]
    for k in range(1, 8):
        yy, cc = half(k)
        partners.append(dev(zl, x, yy, h, cc))
    partners = partners[1:]
    for p in partners:
        pl.semaphore_signal(barrier, inc=1, device_id=p, device_id_type=MESH)
    pl.semaphore_wait(barrier, len(partners))

    sent = []

    def send_c(b):
        src = cot_h.at[0, :, pl.ds(b * CB, CB)]
        dst = cb.at[b, pl.ds(al(slot * TOK, TOK), TOK), :]
        for k in (2, 1, 3):
            sent.append(send(src, dst, s_c.at[b, k - 1], v_c.at[b], to_y(k)))
        pltpu.make_async_copy(src, dst, v_c.at[b]).start()

    def send_a(a):
        dst = xa.at[a, pl.ds(al(slot * TOK, TOK), TOK), :]
        for k in range(1, 8):
            yy, cc = half(k)
            col = al((yy * 4 + (1 - h) * 2 + cc) * ROWS + a * CA, CA)
            sent.append(send(tok_h.at[0, :, pl.ds(col, CA)], dst, s_a.at[a, k - 1], v_a.at[a], dev(zl, x, yy, h, cc)))
        col = al((y * 4 + (1 - h) * 2 + c) * ROWS + a * CA, CA)
        pltpu.make_async_copy(tok_h.at[0, :, pl.ds(col, CA)], dst, v_a.at[a]).start()

    def send_o():
        dst = xo.at[pl.ds(al(slot * TOK, TOK), TOK), :]
        for k in range(1, 8):
            yy, cc = half(k)
            col = al((yy * 4 + h * 2 + cc) * ROWS, ROWS)
            sent.append(send(tok_h.at[0, :, pl.ds(col, ROWS)], dst, s_o.at[k - 1], v_o, dev(zl, x, yy, h, cc)))
        col = al(f * ROWS, ROWS)
        pltpu.make_async_copy(tok_h.at[0, :, pl.ds(col, ROWS)], dst, v_o).start()

    def piece(k):
        return al(lax.rem(zl + 1 + k, 4) * 32, 32)

    def send_r1(k):
        dst = lr.at[x, pl.ds(piece(k), 32), :]
        for d in (2, 1, 3):
            row = al(lax.rem(x + d, 4) * 128 + piece(k), 32)
            sent.append(send(local_h.at[0, pl.ds(row, 32), :], dst, s_r1.at[k, d - 1], v_r1.at[k], to_x(d)))
        row = al(x * 128 + piece(k), 32)
        pltpu.make_async_copy(local_h.at[0, pl.ds(row, 32), :], dst, v_r1.at[k]).start()

    send_c(0)
    for i in range(4):
        send_r1(i)
        send_a(i)
    for b in (1, 2, 3):
        send_c(b)
    send_o()

    pos = pos_ref[0]

    def mask_slot(s, carry):
        first = (lax.rem(s, 4) * 4 + h * 2 + lax.div(s, 4)) * TOK
        place = first + lax.broadcasted_iota(jnp.int32, (TOK, 1), 0)
        hit = jnp.where(pos == place, 1.0, 0.0)
        any_hit = jnp.max(hit, axis=1, keepdims=True)
        mask_v[pl.ds(al(s * TOK, TOK), TOK), :] = jnp.broadcast_to(any_hit, (TOK, 128)).astype(BF)
        return carry

    lax.fori_loop(0, 8, mask_slot, 0)

    emb = emb_ref[...].astype(F32)
    blk = lax.broadcasted_iota(jnp.int32, (16, ROWS), 0)
    theirs = y * 4 + (1 - h) * 2 + c
    ev[0:1, :] = jnp.sum(jnp.where(blk == theirs, emb, 0.0), axis=0, keepdims=True)
    ev[1:2, :] = jnp.sum(jnp.where(blk == f, emb, 0.0), axis=0, keepdims=True)

    load_base.wait()

    def dequant(k):
        await_bytes(lr.at[:, pl.ds(piece(k), 32), :], v_r1.at[k])
        row = al(x * 128 + piece(k), 32)

        def block(i, carry):
            cols = pl.ds(al(i * QBLOCK, QBLOCK), QBLOCK)
            at = base_v[pl.ds(row, 32), cols]
            total = jnp.zeros((32, QBLOCK), F32)
            for s in range(4):
                drift = at - lr[s, pl.ds(piece(k), 32), cols].astype(F32)
                scale = (jnp.max(jnp.abs(drift), axis=1, keepdims=True) + 1e-6).astype(BF).astype(F32)
                code = (drift / scale).astype(BF).astype(F32)
                total = total + code * scale
            if k < 3:
                r2s[k, :, cols] = total.astype(BF)
            else:
                own[:, cols] = total
            return carry

        lax.fori_loop(0, COLS // QBLOCK, block, 0)
        if k < 3:
            sent.append(send(r2s.at[k], r2r.at[k], s_r2.at[k], v_r2.at[k], to_z(k + 1)))

    def forward_c(b):
        mine = pl.ds(al(c * 512, 512), 512)
        await_bytes(cb.at[b, mine, :], v_c.at[b])
        sent.append(send(cb.at[b, mine, :], cb.at[b, mine, :], s_f.at[b], v_f.at[b], other_core))

    def have_c(b):
        theirs_ = pl.ds(al((1 - c) * 512, 512), 512)
        await_bytes(cb.at[b, theirs_, :], v_f.at[b])

    def take_a(a):
        await_bytes(xa.at[a], v_a.at[a])
        fill = jnp.broadcast_to(ev[0:1, a * CA:(a + 1) * CA].astype(BF), (HALF, CA))
        xa[a] = jnp.where(mask_v[...] > 0, fill, xa[a])

    def term(lhs, b):
        return lax.dot_general(lhs, cb[b], (((0,), (0,)), ((), ())), preferred_element_type=F32)

    def partial(a, b):
        ps[b, pl.ds(al(a * CA, CA), CA), :] = term(xa[a], b).astype(BF)

    forward_c(0)
    for a in range(NA):
        dequant(a)
        if a == 0:
            have_c(0)
        take_a(a)
        partial(a, 0)
        part = pl.ds(a * CA, CA)
        sent.append(send(ps.at[0, part, :], pr.at[0, part, :], s_p.at[a], v_p.at[a], antipode))

    def column(b):
        def one(a, carry):
            partial(a, b)
            return carry

        have_c(b)
        lax.fori_loop(0, NA, one, 0)
        sent.append(send(ps.at[b], pr.at[b], s_p.at[3 + b], v_p.at[3 + b], antipode))

    forward_c(1)
    for k in range(3):
        await_bytes(r2r.at[k], v_r2.at[k])
    mine = pl.ds(al(x * 128 + zl * 32, 32), 32)
    total = own[...]
    for k in range(3):
        total = total + r2r[k].astype(F32)
    og[mine, :] = (total * (1.0 / 16.0)).astype(BF)
    for k in (1, 2, 3):
        sent.append(send(og.at[mine, :], og.at[mine, :], s_r3.at[k - 1], v_r3.at[k - 1], to_z(k)))
    column(1)
    forward_c(2)
    column(2)
    forward_c(3)
    for k in (1, 2, 3):
        row = al(x * 128 + lax.rem(zl + 4 - k, 4) * 32, 32)
        await_bytes(og.at[pl.ds(row, 32), :], v_r3.at[k - 1])
    rows_x = pl.ds(al(x * 128, 128), 128)
    for k in (1, 2, 3):
        sent.append(send(og.at[rows_x, :], og.at[rows_x, :], s_r4.at[k - 1], v_r4.at[k - 1], to_x(k)))
    column(3)

    await_bytes(xo, v_o)

    def fill_o(s, carry):
        rows = pl.ds(al(s * TOK, TOK), TOK)
        m = mask_v[rows, :] > 0
        for a in range(NA):
            cols = slice(a * CA, (a + 1) * CA)
            fill = jnp.broadcast_to(ev[1:2, cols].astype(BF), (TOK, CA))
            xo[rows, cols] = jnp.where(m, fill, xo[rows, cols])
        return carry

    lax.fori_loop(0, 8, fill_o, 0)

    def own_term(b, carry):
        for a in range(NA):
            q[b, a * CA:(a + 1) * CA, :] = term(xo[:, a * CA:(a + 1) * CA], b)
        return carry

    lax.fori_loop(0, NB, own_term, 0)

    for k in (1, 2, 3):
        row = al(lax.rem(x + 4 - k, 4) * 128, 128)
        await_bytes(og.at[pl.ds(row, 128), :], v_r4.at[k - 1])
    load_mom.wait()

    def outer(i, carry):
        rows = pl.ds(al(i * 32, 32), 32)
        grad = og[rows, :].astype(F32)
        after = momentum_decay * mom_v[rows, :] + grad
        nm_v[rows, :] = after.astype(BF)
        base_v[rows, :] = base_v[rows, :] - outer_rate * (grad + momentum_decay * after)
        return carry

    lax.fori_loop(0, 16, outer, 0)
    store_nm = pltpu.make_async_copy(nm_v, nm_h, l_sem.at[2])
    store_nm.start()

    for cp in sent:
        cp.wait_send()

    stores = []

    def finish(b, lo, n):
        rows = slice(lo, lo + n)
        cols = slice(b * CB, (b + 1) * CB)
        gradient = (q[b, rows, :] + pr[b, rows, :].astype(F32)) * D ** (-0.5)
        st_v[rows, cols] = (base_v[rows, cols] - inner_rate * gradient).astype(BF)

    for a in range(NA):
        await_bytes(pr.at[0, pl.ds(a * CA, CA), :], v_p.at[a])
        finish(0, a * CA, CA)
    for b in (1, 2, 3):
        await_bytes(pr.at[b], v_p.at[3 + b])
        finish(b, 0, ROWS)
    store_st = pltpu.make_async_copy(st_v, st_h.at[0], l_sem.at[3])
    store_st.start()
    store_nm.wait()
    store_st.wait()


def body(base, local, momentum, tokens, mask_embed, mask_pos, cotangent):
    hbm = pl.BlockSpec(memory_space=pl.ANY)
    vmem = pl.BlockSpec(memory_space=pltpu.VMEM)
    dma = pltpu.SemaphoreType.DMA
    new_momentum, stepped = pl.pallas_call(
        kernel,
        name="step",
        out_shape=(
            jax.ShapeDtypeStruct((ROWS, COLS), BF),
            jax.ShapeDtypeStruct((1, ROWS, COLS), BF),
        ),
        in_specs=[hbm, hbm, hbm, hbm, vmem, vmem, hbm],
        out_specs=(hbm, hbm),
        scratch_shapes=[
            pltpu.VMEM((ROWS, COLS), F32),
            pltpu.VMEM((ROWS, COLS), F32),
            pltpu.VMEM((4, 128, COLS), BF),
            pltpu.VMEM((3, 32, COLS), BF),
            pltpu.VMEM((3, 32, COLS), BF),
            pltpu.VMEM((32, COLS), F32),
            pltpu.VMEM((ROWS, COLS), BF),
            pltpu.VMEM((NA, HALF, CA), BF),
            pltpu.VMEM((HALF, ROWS), BF),
            pltpu.VMEM((NB, HALF, CB), BF),
            pltpu.VMEM((HALF, 128), BF),
            pltpu.VMEM((8, ROWS), F32),
            pltpu.VMEM((NB, ROWS, CB), BF),
            pltpu.VMEM((NB, ROWS, CB), BF),
            pltpu.VMEM((NB, ROWS, CB), F32),
            pltpu.VMEM((ROWS, COLS), BF),
            pltpu.VMEM((ROWS, COLS), BF),
            dma((NB, 3)),
            dma((NB,)),
            dma((NA, 7)),
            dma((7,)),
            dma((7,)),
            dma((4, 3)),
            dma((3,)),
            dma((3,)),
            dma((3,)),
            dma((NB,)),
            dma((NB,)),
            dma((NA,)),
            dma(()),
            dma((7,)),
            dma((4,)),
            dma((3,)),
            dma((3,)),
            dma((3,)),
            dma((4,)),
        ],
        compiler_params=pltpu.CompilerParams(
            collective_id=0, has_side_effects=True, vmem_limit_bytes=48 * 2**20
        ),
    )(base, local, momentum, tokens, mask_embed.reshape(16, ROWS), mask_pos, cotangent)
    return new_momentum, stepped


def solution(mesh):
    in_specs = (
        P("fsdp", None),
        P("replica", "fsdp", None),
        P("fsdp", None),
        P("replica", "fsdp", None),
        P(),
        P("replica", None, None),
        P("replica", "fsdp", None),
    )
    out_specs = (P("fsdp", None), P("replica", "fsdp", None))
    return jax.shard_map(body, mesh=mesh, in_specs=in_specs, out_specs=out_specs, check_vma=False)
```

```python
import jax
import jax.numpy as jnp
from jax import lax
from jax.experimental import pallas as pl
from jax.experimental.pallas import tpu as pltpu
from jax.sharding import PartitionSpec as P

D = 8192
ROWS = 512
COLS = 1024
TOK = 128
QBLOCK = 128
NB = 4
CB = COLS // NB
NA = 4
CA = ROWS // NA
HALF = 1024

momentum_decay = 0.9
outer_rate = 0.7
inner_rate = 0.5

MESH = pl.DeviceIdType.MESH
BF = jnp.bfloat16
F32 = jnp.float32


def al(v, m):
    return pl.multiple_of(v, m)


def kernel(base_h, local_h, mom_h, tok_h, emb_ref, pos_h, cot_h, nm_v, st_v,
           base_v, mom_v, lr, r2s, r2r, own, og, xa, xo, cb, mask_v, ev, ps, pr, q, pos_v,
           s_c, s_f, s_a, s_o, s_p, s_r1, s_r2, s_r3, s_r4,
           v_c, v_f, v_a, v_o, v_p, v_r1, v_r2, v_r3, v_r4, l_sem):
    r = lax.axis_index("replica")
    f = lax.axis_index("fsdp")
    zl, x = lax.div(r, 4), lax.rem(r, 4)
    y, h, c = lax.div(f, 4), lax.rem(lax.div(f, 2), 2), lax.rem(f, 2)
    slot = c * 4 + y

    def dev(zl_, x_, y_, h_, c_):
        return {"replica": zl_ * 4 + x_, "fsdp": y_ * 4 + h_ * 2 + c_}

    def half(k):
        t = lax.rem(slot + k, 8)
        return lax.rem(t, 4), lax.div(t, 4)

    def to_y(k):
        return dev(zl, x, lax.rem(y + k, 4), h, c)

    def to_x(k):
        return dev(zl, lax.rem(x + k, 4), y, h, c)

    def to_z(k):
        return dev(lax.rem(zl + k, 4), x, y, h, c)

    other_core = dev(zl, x, y, h, 1 - c)
    antipode = dev(zl, x, y, 1 - h, c)

    def send(src, dst, ss, rs, to):
        cp = pltpu.make_async_remote_copy(
            src_ref=src, dst_ref=dst, send_sem=ss, recv_sem=rs, device_id=to, device_id_type=MESH
        )
        cp.start()
        return cp

    def await_bytes(ref, sem):
        pltpu.make_async_copy(ref, ref, sem).wait()

    load_base = pltpu.make_async_copy(base_h, base_v, l_sem.at[0])
    load_mom = pltpu.make_async_copy(mom_h, mom_v, l_sem.at[1])
    load_pos = pltpu.make_async_copy(pos_h, pos_v, l_sem.at[2])
    load_pos.start()
    load_base.start()
    load_mom.start()

    barrier = pltpu.get_barrier_semaphore()
    partners = [other_core, antipode]
    for k in (1, 2, 3):
        partners += [to_x(k), to_z(k)]
    for k in range(1, 8):
        yy, cc = half(k)
        partners.append(dev(zl, x, yy, h, cc))
    partners = partners[1:]
    for p in partners:
        pl.semaphore_signal(barrier, inc=1, device_id=p, device_id_type=MESH)
    pl.semaphore_wait(barrier, len(partners))

    sent = []

    def send_c(b):
        src = cot_h.at[0, :, pl.ds(b * CB, CB)]
        dst = cb.at[b, pl.ds(al(slot * TOK, TOK), TOK), :]
        for k in (2, 1, 3):
            sent.append(send(src, dst, s_c.at[b, k - 1], v_c.at[b], to_y(k)))
        pltpu.make_async_copy(src, dst, v_c.at[b]).start()

    def send_a(a):
        dst = xa.at[a, pl.ds(al(slot * TOK, TOK), TOK), :]
        for k in range(1, 8):
            yy, cc = half(k)
            col = al((yy * 4 + (1 - h) * 2 + cc) * ROWS + a * CA, CA)
            sent.append(send(tok_h.at[0, :, pl.ds(col, CA)], dst, s_a.at[a, k - 1], v_a.at[a], dev(zl, x, yy, h, cc)))
        col = al((y * 4 + (1 - h) * 2 + c) * ROWS + a * CA, CA)
        pltpu.make_async_copy(tok_h.at[0, :, pl.ds(col, CA)], dst, v_a.at[a]).start()

    def send_o():
        dst = xo.at[pl.ds(al(slot * TOK, TOK), TOK), :]
        for k in range(1, 8):
            yy, cc = half(k)
            col = al((yy * 4 + h * 2 + cc) * ROWS, ROWS)
            sent.append(send(tok_h.at[0, :, pl.ds(col, ROWS)], dst, s_o.at[k - 1], v_o, dev(zl, x, yy, h, cc)))
        col = al(f * ROWS, ROWS)
        pltpu.make_async_copy(tok_h.at[0, :, pl.ds(col, ROWS)], dst, v_o).start()

    def piece(k):
        return al(lax.rem(zl + 1 + k, 4) * 32, 32)

    def send_r1(k):
        dst = lr.at[x, pl.ds(piece(k), 32), :]
        for d in (2, 1, 3):
            row = al(lax.rem(x + d, 4) * 128 + piece(k), 32)
            sent.append(send(local_h.at[0, pl.ds(row, 32), :], dst, s_r1.at[k, d - 1], v_r1.at[k], to_x(d)))
        row = al(x * 128 + piece(k), 32)
        pltpu.make_async_copy(local_h.at[0, pl.ds(row, 32), :], dst, v_r1.at[k]).start()

    send_c(0)
    for i in range(4):
        send_r1(i)
        send_a(i)
    for b in (1, 2, 3):
        send_c(b)
    send_o()

    load_pos.wait()
    pos = pos_v[0]

    def mask_slot(s, carry):
        first = (lax.rem(s, 4) * 4 + h * 2 + lax.div(s, 4)) * TOK
        place = first + lax.broadcasted_iota(jnp.int32, (TOK, 1), 0)
        hit = jnp.where(pos == place, 1.0, 0.0)
        any_hit = jnp.max(hit, axis=1, keepdims=True)
        mask_v[pl.ds(al(s * TOK, TOK), TOK), :] = jnp.broadcast_to(any_hit, (TOK, 128)).astype(BF)
        return carry

    lax.fori_loop(0, 8, mask_slot, 0)

    emb = emb_ref[...].astype(F32)
    blk = lax.broadcasted_iota(jnp.int32, (16, ROWS), 0)
    theirs = y * 4 + (1 - h) * 2 + c
    ev[0:1, :] = jnp.sum(jnp.where(blk == theirs, emb, 0.0), axis=0, keepdims=True)
    ev[1:2, :] = jnp.sum(jnp.where(blk == f, emb, 0.0), axis=0, keepdims=True)

    load_base.wait()

    def dequant(k):
        await_bytes(lr.at[:, pl.ds(piece(k), 32), :], v_r1.at[k])
        row = al(x * 128 + piece(k), 32)

        def block(i, carry):
            cols = pl.ds(al(i * QBLOCK, QBLOCK), QBLOCK)
            at = base_v[pl.ds(row, 32), cols]
            total = jnp.zeros((32, QBLOCK), F32)
            for s in range(4):
                drift = at - lr[s, pl.ds(piece(k), 32), cols].astype(F32)
                scale = (jnp.max(jnp.abs(drift), axis=1, keepdims=True) + 1e-6).astype(BF).astype(F32)
                code = (drift / scale).astype(BF).astype(F32)
                total = total + code * scale
            if k < 3:
                r2s[k, :, cols] = total.astype(BF)
            else:
                own[:, cols] = total
            return carry

        lax.fori_loop(0, COLS // QBLOCK, block, 0)
        if k < 3:
            sent.append(send(r2s.at[k], r2r.at[k], s_r2.at[k], v_r2.at[k], to_z(k + 1)))

    def forward_c(b):
        mine = pl.ds(al(c * 512, 512), 512)
        await_bytes(cb.at[b, mine, :], v_c.at[b])
        sent.append(send(cb.at[b, mine, :], cb.at[b, mine, :], s_f.at[b], v_f.at[b], other_core))

    def have_c(b):
        theirs_ = pl.ds(al((1 - c) * 512, 512), 512)
        await_bytes(cb.at[b, theirs_, :], v_f.at[b])

    def take_a(a):
        await_bytes(xa.at[a], v_a.at[a])
        fill = jnp.broadcast_to(ev[0:1, a * CA:(a + 1) * CA].astype(BF), (HALF, CA))
        xa[a] = jnp.where(mask_v[...] > 0, fill, xa[a])

    def term(lhs, b):
        return lax.dot_general(lhs, cb[b], (((0,), (0,)), ((), ())), preferred_element_type=F32)

    def partial(a, b):
        ps[b, pl.ds(al(a * CA, CA), CA), :] = term(xa[a], b).astype(BF)

    forward_c(0)
    for a in range(NA):
        dequant(a)
        if a == 0:
            have_c(0)
        take_a(a)
        partial(a, 0)
        part = pl.ds(a * CA, CA)
        send(ps.at[0, part, :], pr.at[0, part, :], s_p.at[0, a], v_p.at[0, a], antipode)

    def column(b):
        def one(a, carry):
            partial(a, b)
            rows = pl.ds(al(a * CA, CA), CA)
            send(ps.at[b, rows, :], pr.at[b, rows, :], s_p.at[b, a], v_p.at[b, a], antipode)
            return carry

        have_c(b)
        lax.fori_loop(0, NA, one, 0)

    forward_c(1)
    column(1)
    for k in range(3):
        await_bytes(r2r.at[k], v_r2.at[k])
    mine = pl.ds(al(x * 128 + zl * 32, 32), 32)
    total = own[...]
    for k in range(3):
        total = total + r2r[k].astype(F32)
    og[mine, :] = (total * (1.0 / 16.0)).astype(BF)
    for k in (1, 2, 3):
        sent.append(send(og.at[mine, :], og.at[mine, :], s_r3.at[k - 1], v_r3.at[k - 1], to_z(k)))
    forward_c(2)
    forward_c(3)
    for k in (1, 2, 3):
        row = al(x * 128 + lax.rem(zl + 4 - k, 4) * 32, 32)
        await_bytes(og.at[pl.ds(row, 32), :], v_r3.at[k - 1])
    rows_x = pl.ds(al(x * 128, 128), 128)
    for k in (1, 2, 3):
        sent.append(send(og.at[rows_x, :], og.at[rows_x, :], s_r4.at[k - 1], v_r4.at[k - 1], to_x(k)))

    column(2)
    column(3)
    await_bytes(xo, v_o)

    def fill_o(s, carry):
        rows = pl.ds(al(s * TOK, TOK), TOK)
        m = mask_v[rows, :] > 0
        for a in range(NA):
            cols = slice(a * CA, (a + 1) * CA)
            fill = jnp.broadcast_to(ev[1:2, cols].astype(BF), (TOK, CA))
            xo[rows, cols] = jnp.where(m, fill, xo[rows, cols])
        return carry

    lax.fori_loop(0, 8, fill_o, 0)

    def own_term(b, carry):
        for a in range(NA):
            q[b, a * CA:(a + 1) * CA, :] = term(xo[:, a * CA:(a + 1) * CA], b)
        return carry

    lax.fori_loop(0, NB, own_term, 0)

    for k in (1, 2, 3):
        row = al(lax.rem(x + 4 - k, 4) * 128, 128)
        await_bytes(og.at[pl.ds(row, 128), :], v_r4.at[k - 1])
    load_mom.wait()

    def outer(i, carry):
        rows = pl.ds(al(i * 32, 32), 32)
        grad = og[rows, :].astype(F32)
        after = momentum_decay * mom_v[rows, :] + grad
        nm_v[rows, :] = after.astype(BF)
        base_v[rows, :] = base_v[rows, :] - outer_rate * (grad + momentum_decay * after)
        return carry

    lax.fori_loop(0, 16, outer, 0)

    for cp in sent:
        cp.wait_send()

    def finish(b, lo, n):
        rows = slice(lo, lo + n)
        cols = slice(b * CB, (b + 1) * CB)
        gradient = (q[b, rows, :] + pr[b, rows, :].astype(F32)) * D ** (-0.5)
        st_v[0, rows, cols] = (base_v[rows, cols] - inner_rate * gradient).astype(BF)

    for b in range(NB):
        for a in range(NA):
            part = pl.ds(a * CA, CA)
            await_bytes(pr.at[b, part, :], v_p.at[b, a])
            finish(b, a * CA, CA)
            await_bytes(ps.at[b, part, :], s_p.at[b, a])


def body(base, local, momentum, tokens, mask_embed, mask_pos, cotangent):
    hbm = pl.BlockSpec(memory_space=pltpu.HBM)
    vmem = pl.BlockSpec(memory_space=pltpu.VMEM)
    dma = pltpu.SemaphoreType.DMA
    new_momentum, stepped = pl.pallas_call(
        kernel,
        name="step",
        out_shape=(
            jax.ShapeDtypeStruct((ROWS, COLS), BF),
            jax.ShapeDtypeStruct((1, ROWS, COLS), BF),
        ),
        in_specs=[hbm, hbm, hbm, hbm, vmem, hbm, hbm],
        out_specs=(vmem, vmem),
        scratch_shapes=[
            pltpu.VMEM((ROWS, COLS), F32),
            pltpu.VMEM((ROWS, COLS), F32),
            pltpu.VMEM((4, 128, COLS), BF),
            pltpu.VMEM((3, 32, COLS), BF),
            pltpu.VMEM((3, 32, COLS), BF),
            pltpu.VMEM((32, COLS), F32),
            pltpu.VMEM((ROWS, COLS), BF),
            pltpu.VMEM((NA, HALF, CA), BF),
            pltpu.VMEM((HALF, ROWS), BF),
            pltpu.VMEM((NB, HALF, CB), BF),
            pltpu.VMEM((HALF, 128), BF),
            pltpu.VMEM((8, ROWS), F32),
            pltpu.VMEM((NB, ROWS, CB), BF),
            pltpu.VMEM((NB, ROWS, CB), BF),
            pltpu.VMEM((NB, ROWS, CB), F32),
            pltpu.VMEM((1, 1, 768), jnp.int32),
            dma((NB, 3)),
            dma((NB,)),
            dma((NA, 7)),
            dma((7,)),
            dma((NB, NA)),
            dma((4, 3)),
            dma((3,)),
            dma((3,)),
            dma((3,)),
            dma((NB,)),
            dma((NB,)),
            dma((NA,)),
            dma(()),
            dma((NB, NA)),
            dma((4,)),
            dma((3,)),
            dma((3,)),
            dma((3,)),
            dma((3,)),
        ],
        compiler_params=pltpu.CompilerParams(
            collective_id=0, has_side_effects=True, vmem_limit_bytes=60 * 2**20
        ),
    )(base, local, momentum, tokens, mask_embed.reshape(16, ROWS), mask_pos, cotangent)
    return new_momentum, stepped


def solution(mesh):
    in_specs = (
        P("fsdp", None),
        P("replica", "fsdp", None),
        P("fsdp", None),
        P("replica", "fsdp", None),
        P(),
        P("replica", None, None),
        P("replica", "fsdp", None),
    )
    out_specs = (P("fsdp", None), P("replica", "fsdp", None))
    return jax.shard_map(body, mesh=mesh, in_specs=in_specs, out_specs=out_specs, check_vma=False)
```

```python
import jax
import jax.numpy as jnp
from jax import lax
from jax.experimental import pallas as pl
from jax.experimental.pallas import tpu as pltpu
from jax.sharding import PartitionSpec as P

D = 8192
ROWS = 512
COLS = 1024
TOK = 128
QBLOCK = 128
NB = 4
CB = COLS // NB
NA = 4
CA = ROWS // NA
HALF = 1024

momentum_decay = 0.9
outer_rate = 0.7
inner_rate = 0.5

MESH = pl.DeviceIdType.MESH
BF = jnp.bfloat16
F32 = jnp.float32


def al(v, m):
    return pl.multiple_of(v, m)


def kernel(base_h, local_h, mom_h, tok_h, emb_h, pos_h, cot_h, nm_v, st_v,
           base_v, mom_v, lr, r2s, r2r, own, og, xa, xo, cb, mask_v, ev, ps, pr, q, pos_v, emb_v,
           s_c, s_f, s_a, s_o, s_p, s_r1, s_r2, s_r3, s_r4,
           v_c, v_f, v_a, v_o, v_p, v_r1, v_r2, v_r3, v_r4, l_sem):
    r = lax.axis_index("replica")
    f = lax.axis_index("fsdp")
    zl, x = lax.div(r, 4), lax.rem(r, 4)
    y, h, c = lax.div(f, 4), lax.rem(lax.div(f, 2), 2), lax.rem(f, 2)
    slot = c * 4 + y

    def dev(zl_, x_, y_, h_, c_):
        return {"replica": zl_ * 4 + x_, "fsdp": y_ * 4 + h_ * 2 + c_}

    def half(k):
        t = lax.rem(slot + k, 8)
        return lax.rem(t, 4), lax.div(t, 4)

    def to_y(k):
        return dev(zl, x, lax.rem(y + k, 4), h, c)

    def to_x(k):
        return dev(zl, lax.rem(x + k, 4), y, h, c)

    def to_z(k):
        return dev(lax.rem(zl + k, 4), x, y, h, c)

    other_core = dev(zl, x, y, h, 1 - c)
    antipode = dev(zl, x, y, 1 - h, c)

    def send(src, dst, ss, rs, to):
        cp = pltpu.make_async_remote_copy(
            src_ref=src, dst_ref=dst, send_sem=ss, recv_sem=rs, device_id=to, device_id_type=MESH
        )
        cp.start()
        return cp

    def await_bytes(ref, sem):
        pltpu.make_async_copy(ref, ref, sem).wait()

    load_base = pltpu.make_async_copy(base_h, base_v, l_sem.at[0])
    load_mom = pltpu.make_async_copy(mom_h, mom_v, l_sem.at[1])
    load_pos = pltpu.make_async_copy(pos_h, pos_v, l_sem.at[2])
    load_pos.start()
    load_emb = pltpu.make_async_copy(emb_h, emb_v, l_sem.at[3])
    load_emb.start()
    load_base.start()
    load_mom.start()

    barrier = pltpu.get_barrier_semaphore()
    partners = [other_core, antipode]
    for k in (1, 2, 3):
        partners += [to_x(k), to_z(k)]
    for k in range(1, 8):
        yy, cc = half(k)
        partners.append(dev(zl, x, yy, h, cc))
    partners = partners[1:]
    for p in partners:
        pl.semaphore_signal(barrier, inc=1, device_id=p, device_id_type=MESH)
    pl.semaphore_wait(barrier, len(partners))

    sent = []

    def send_c(b):
        src = cot_h.at[0, :, pl.ds(b * CB, CB)]
        dst = cb.at[b, pl.ds(al(slot * TOK, TOK), TOK), :]
        for k in (2, 1, 3):
            sent.append(send(src, dst, s_c.at[b, k - 1], v_c.at[b], to_y(k)))
        pltpu.make_async_copy(src, dst, v_c.at[b]).start()

    def send_a(a):
        dst = xa.at[a, pl.ds(al(slot * TOK, TOK), TOK), :]
        for k in range(1, 8):
            yy, cc = half(k)
            col = al((yy * 4 + (1 - h) * 2 + cc) * ROWS + a * CA, CA)
            sent.append(send(tok_h.at[0, :, pl.ds(col, CA)], dst, s_a.at[a, k - 1], v_a.at[a], dev(zl, x, yy, h, cc)))
        col = al((y * 4 + (1 - h) * 2 + c) * ROWS + a * CA, CA)
        pltpu.make_async_copy(tok_h.at[0, :, pl.ds(col, CA)], dst, v_a.at[a]).start()

    def send_o():
        dst = xo.at[pl.ds(al(slot * TOK, TOK), TOK), :]
        for k in range(1, 8):
            yy, cc = half(k)
            col = al((yy * 4 + h * 2 + cc) * ROWS, ROWS)
            sent.append(send(tok_h.at[0, :, pl.ds(col, ROWS)], dst, s_o.at[k - 1], v_o, dev(zl, x, yy, h, cc)))
        col = al(f * ROWS, ROWS)
        pltpu.make_async_copy(tok_h.at[0, :, pl.ds(col, ROWS)], dst, v_o).start()

    def piece(k):
        return al(lax.rem(zl + 1 + k, 4) * 32, 32)

    def send_r1(k):
        dst = lr.at[x, pl.ds(piece(k), 32), :]
        for d in (2, 1, 3):
            row = al(lax.rem(x + d, 4) * 128 + piece(k), 32)
            sent.append(send(local_h.at[0, pl.ds(row, 32), :], dst, s_r1.at[k, d - 1], v_r1.at[k], to_x(d)))
        row = al(x * 128 + piece(k), 32)
        pltpu.make_async_copy(local_h.at[0, pl.ds(row, 32), :], dst, v_r1.at[k]).start()

    send_c(0)
    for i in range(4):
        send_r1(i)
        send_a(i)
    for b in (1, 2, 3):
        send_c(b)
    send_o()

    load_pos.wait()
    pos = pos_v[0]

    def mask_slot(s, carry):
        first = (lax.rem(s, 4) * 4 + h * 2 + lax.div(s, 4)) * TOK
        place = first + lax.broadcasted_iota(jnp.int32, (TOK, 1), 0)
        hit = jnp.where(pos == place, 1.0, 0.0)
        any_hit = jnp.max(hit, axis=1, keepdims=True)
        mask_v[pl.ds(al(s * TOK, TOK), TOK), :] = jnp.broadcast_to(any_hit, (TOK, 128)).astype(BF)
        return carry

    lax.fori_loop(0, 8, mask_slot, 0)

    load_emb.wait()
    emb = emb_v[...].astype(F32)
    line = lax.broadcasted_iota(jnp.int32, (64, 128), 0)
    theirs = y * 4 + (1 - h) * 2 + c
    for a in range(NA):
        cols = slice(a * CA, (a + 1) * CA)
        ev[0:1, cols] = jnp.sum(jnp.where(line == theirs * NA + a, emb, 0.0), axis=0, keepdims=True)
        ev[1:2, cols] = jnp.sum(jnp.where(line == f * NA + a, emb, 0.0), axis=0, keepdims=True)

    load_base.wait()

    def dequant(k):
        await_bytes(lr.at[:, pl.ds(piece(k), 32), :], v_r1.at[k])
        row = al(x * 128 + piece(k), 32)

        def block(i, carry):
            cols = pl.ds(al(i * QBLOCK, QBLOCK), QBLOCK)
            at = base_v[pl.ds(row, 32), cols]
            total = jnp.zeros((32, QBLOCK), F32)
            for s in range(4):
                drift = at - lr[s, pl.ds(piece(k), 32), cols].astype(F32)
                scale = (jnp.max(jnp.abs(drift), axis=1, keepdims=True) + 1e-6).astype(BF).astype(F32)
                code = (drift / scale).astype(BF).astype(F32)
                total = total + code * scale
            if k < 3:
                r2s[k, :, cols] = total.astype(BF)
            else:
                own[:, cols] = total
            return carry

        lax.fori_loop(0, COLS // QBLOCK, block, 0)
        if k < 3:
            sent.append(send(r2s.at[k], r2r.at[k], s_r2.at[k], v_r2.at[k], to_z(k + 1)))

    def forward_c(b):
        mine = pl.ds(al(c * 512, 512), 512)
        await_bytes(cb.at[b, mine, :], v_c.at[b])
        sent.append(send(cb.at[b, mine, :], cb.at[b, mine, :], s_f.at[b], v_f.at[b], other_core))

    def have_c(b):
        theirs_ = pl.ds(al((1 - c) * 512, 512), 512)
        await_bytes(cb.at[b, theirs_, :], v_f.at[b])

    def take_a(a):
        await_bytes(xa.at[a], v_a.at[a])
        fill = jnp.broadcast_to(ev[0:1, a * CA:(a + 1) * CA].astype(BF), (HALF, CA))
        xa[a] = jnp.where(mask_v[...] > 0, fill, xa[a])

    def term(lhs, b):
        return lax.dot_general(lhs, cb[b], (((0,), (0,)), ((), ())), preferred_element_type=F32)

    def partial(a, b):
        ps[b, pl.ds(al(a * CA, CA), CA), :] = term(xa[a], b).astype(BF)

    forward_c(0)
    for a in range(NA):
        dequant(a)
        if a == 0:
            have_c(0)
        take_a(a)
        partial(a, 0)
        part = pl.ds(a * CA, CA)
        send(ps.at[0, part, :], pr.at[0, part, :], s_p.at[0, a], v_p.at[0, a], antipode)

    def column(b):
        def one(a, carry):
            partial(a, b)
            rows = pl.ds(al(a * CA, CA), CA)
            send(ps.at[b, rows, :], pr.at[b, rows, :], s_p.at[b, a], v_p.at[b, a], antipode)
            return carry

        have_c(b)
        lax.fori_loop(0, NA, one, 0)

    forward_c(1)
    column(1)
    for k in range(3):
        await_bytes(r2r.at[k], v_r2.at[k])
    mine = pl.ds(al(x * 128 + zl * 32, 32), 32)
    total = own[...]
    for k in range(3):
        total = total + r2r[k].astype(F32)
    og[mine, :] = (total * (1.0 / 16.0)).astype(BF)
    for k in (1, 2, 3):
        sent.append(send(og.at[mine, :], og.at[mine, :], s_r3.at[k - 1], v_r3.at[k - 1], to_z(k)))
    forward_c(2)
    forward_c(3)
    for k in (1, 2, 3):
        row = al(x * 128 + lax.rem(zl + 4 - k, 4) * 32, 32)
        await_bytes(og.at[pl.ds(row, 32), :], v_r3.at[k - 1])
    rows_x = pl.ds(al(x * 128, 128), 128)
    for k in (1, 2, 3):
        sent.append(send(og.at[rows_x, :], og.at[rows_x, :], s_r4.at[k - 1], v_r4.at[k - 1], to_x(k)))

    column(2)
    column(3)
    await_bytes(xo, v_o)

    def fill_o(s, carry):
        rows = pl.ds(al(s * TOK, TOK), TOK)
        m = mask_v[rows, :] > 0
        for a in range(NA):
            cols = slice(a * CA, (a + 1) * CA)
            fill = jnp.broadcast_to(ev[1:2, cols].astype(BF), (TOK, CA))
            xo[rows, cols] = jnp.where(m, fill, xo[rows, cols])
        return carry

    lax.fori_loop(0, 8, fill_o, 0)

    def own_term(b, carry):
        for a in range(NA):
            q[b, a * CA:(a + 1) * CA, :] = term(xo[:, a * CA:(a + 1) * CA], b)
        return carry

    lax.fori_loop(0, NB, own_term, 0)

    for k in (1, 2, 3):
        row = al(lax.rem(x + 4 - k, 4) * 128, 128)
        await_bytes(og.at[pl.ds(row, 128), :], v_r4.at[k - 1])
    load_mom.wait()

    def outer(i, carry):
        rows = pl.ds(al(i * 32, 32), 32)
        grad = og[rows, :].astype(F32)
        after = momentum_decay * mom_v[rows, :] + grad
        nm_v[rows, :] = after.astype(BF)
        base_v[rows, :] = base_v[rows, :] - outer_rate * (grad + momentum_decay * after)
        return carry

    lax.fori_loop(0, 16, outer, 0)

    for cp in sent:
        cp.wait_send()

    def finish(b, lo, n):
        rows = slice(lo, lo + n)
        cols = slice(b * CB, (b + 1) * CB)
        gradient = (q[b, rows, :] + pr[b, rows, :].astype(F32)) * D ** (-0.5)
        st_v[0, rows, cols] = (base_v[rows, cols] - inner_rate * gradient).astype(BF)

    for b in range(NB):
        for a in range(NA):
            part = pl.ds(a * CA, CA)
            await_bytes(pr.at[b, part, :], v_p.at[b, a])
            finish(b, a * CA, CA)
            await_bytes(ps.at[b, part, :], s_p.at[b, a])


def body(base, local, momentum, tokens, mask_embed, mask_pos, cotangent):
    hbm = pl.BlockSpec(memory_space=pltpu.HBM)
    dma = pltpu.SemaphoreType.DMA
    new_momentum, stepped = pl.pallas_call(
        kernel,
        name="step",
        out_shape=(
            pltpu.VMEM((ROWS, COLS), BF),
            pltpu.VMEM((1, ROWS, COLS), BF),
        ),
        in_specs=[hbm] * 7,
        out_specs=(pl.BlockSpec(memory_space=pltpu.VMEM),) * 2,
        scratch_shapes=[
            pltpu.VMEM((ROWS, COLS), F32),
            pltpu.VMEM((ROWS, COLS), F32),
            pltpu.VMEM((4, 128, COLS), BF),
            pltpu.VMEM((3, 32, COLS), BF),
            pltpu.VMEM((3, 32, COLS), BF),
            pltpu.VMEM((32, COLS), F32),
            pltpu.VMEM((ROWS, COLS), BF),
            pltpu.VMEM((NA, HALF, CA), BF),
            pltpu.VMEM((HALF, ROWS), BF),
            pltpu.VMEM((NB, HALF, CB), BF),
            pltpu.VMEM((HALF, 128), BF),
            pltpu.VMEM((8, ROWS), F32),
            pltpu.VMEM((NB, ROWS, CB), BF),
            pltpu.VMEM((NB, ROWS, CB), BF),
            pltpu.VMEM((NB, ROWS, CB), F32),
            pltpu.VMEM((1, 1, 768), jnp.int32),
            pltpu.VMEM((64, 128), BF),
            dma((NB, 3)),
            dma((NB,)),
            dma((NA, 7)),
            dma((7,)),
            dma((NB, NA)),
            dma((4, 3)),
            dma((3,)),
            dma((3,)),
            dma((3,)),
            dma((NB,)),
            dma((NB,)),
            dma((NA,)),
            dma(()),
            dma((NB, NA)),
            dma((4,)),
            dma((3,)),
            dma((3,)),
            dma((3,)),
            dma((4,)),
        ],
        compiler_params=pltpu.CompilerParams(
            collective_id=0, has_side_effects=True, vmem_limit_bytes=60 * 2**20
        ),
    )(base, local, momentum, tokens, mask_embed.reshape(64, 128), mask_pos, cotangent)
    return new_momentum, stepped


def solution(mesh):
    in_specs = (
        P("fsdp", None),
        P("replica", "fsdp", None),
        P("fsdp", None),
        P("replica", "fsdp", None),
        P(),
        P("replica", None, None),
        P("replica", "fsdp", None),
    )
    out_specs = (P("fsdp", None), P("replica", "fsdp", None))
    return jax.shard_map(body, mesh=mesh, in_specs=in_specs, out_specs=out_specs, check_vma=False)
```

```python
import jax
import jax.numpy as jnp
from jax import lax
from jax.experimental import pallas as pl
from jax.experimental.pallas import tpu as pltpu
from jax.sharding import PartitionSpec as P

D = 8192
ROWS = 512
COLS = 1024
TOK = 128
QBLOCK = 128
NB = 4
CB = COLS // NB
NA = 4
CA = ROWS // NA
HALF = 1024

momentum_decay = 0.9
outer_rate = 0.7
inner_rate = 0.5

MESH = pl.DeviceIdType.MESH
BF = jnp.bfloat16
F32 = jnp.float32


def al(v, m):
    return pl.multiple_of(v, m)


def kernel(base_h, local_h, mom_h, tok_h, emb_h, pos_h, cot_h, nm_v, st_v,
           base_v, mom_v, lr, r2s, r2r, own, og, xa, xo, cb, mask_v, ev, ps, pr, q, pos_v, emb_v,
           s_c, s_f, s_a, s_o, s_p, s_r1, s_r2, s_r3, s_r4,
           v_c, v_f, v_a, v_o, v_p, v_r1, v_r2, v_r3, v_r4, l_sem):
    r = lax.axis_index("replica")
    f = lax.axis_index("fsdp")
    zl, x = lax.div(r, 4), lax.rem(r, 4)
    y, h, c = lax.div(f, 4), lax.rem(lax.div(f, 2), 2), lax.rem(f, 2)
    slot = c * 4 + y

    def dev(zl_, x_, y_, h_, c_):
        return {"replica": zl_ * 4 + x_, "fsdp": y_ * 4 + h_ * 2 + c_}

    def half(k):
        t = lax.rem(slot + k, 8)
        return lax.rem(t, 4), lax.div(t, 4)

    def to_y(k):
        return dev(zl, x, lax.rem(y + k, 4), h, c)

    def to_x(k):
        return dev(zl, lax.rem(x + k, 4), y, h, c)

    def to_z(k):
        return dev(lax.rem(zl + k, 4), x, y, h, c)

    other_core = dev(zl, x, y, h, 1 - c)
    antipode = dev(zl, x, y, 1 - h, c)

    def send(src, dst, ss, rs, to):
        cp = pltpu.make_async_remote_copy(
            src_ref=src, dst_ref=dst, send_sem=ss, recv_sem=rs, device_id=to, device_id_type=MESH
        )
        cp.start()
        return cp

    def await_bytes(ref, sem):
        pltpu.make_async_copy(ref, ref, sem).wait()

    load_base = pltpu.make_async_copy(base_h, base_v, l_sem.at[0])
    load_mom = pltpu.make_async_copy(mom_h, mom_v, l_sem.at[1])
    load_pos = pltpu.make_async_copy(pos_h, pos_v, l_sem.at[2])
    load_pos.start()
    load_emb = pltpu.make_async_copy(emb_h, emb_v, l_sem.at[3])
    load_emb.start()
    load_base.start()
    load_mom.start()

    barrier = pltpu.get_barrier_semaphore()
    partners = [other_core, antipode]
    for k in (1, 2, 3):
        partners += [to_x(k), to_z(k)]
    for k in range(1, 8):
        yy, cc = half(k)
        partners.append(dev(zl, x, yy, h, cc))
    partners = partners[1:]
    for p in partners:
        pl.semaphore_signal(barrier, inc=1, device_id=p, device_id_type=MESH)
    pl.semaphore_wait(barrier, len(partners))

    sent = []

    def send_c(b):
        src = cot_h.at[0, :, pl.ds(b * CB, CB)]
        dst = cb.at[b, pl.ds(al(slot * TOK, TOK), TOK), :]
        for k in (2, 1, 3):
            sent.append(send(src, dst, s_c.at[b, k - 1], v_c.at[b], to_y(k)))
        pltpu.make_async_copy(src, dst, v_c.at[b]).start()

    def send_a(a):
        dst = xa.at[a, pl.ds(al(slot * TOK, TOK), TOK), :]
        for k in range(1, 8):
            yy, cc = half(k)
            col = al((yy * 4 + (1 - h) * 2 + cc) * ROWS + a * CA, CA)
            sent.append(send(tok_h.at[0, :, pl.ds(col, CA)], dst, s_a.at[a, k - 1], v_a.at[a], dev(zl, x, yy, h, cc)))
        col = al((y * 4 + (1 - h) * 2 + c) * ROWS + a * CA, CA)
        pltpu.make_async_copy(tok_h.at[0, :, pl.ds(col, CA)], dst, v_a.at[a]).start()

    def send_o():
        dst = xo.at[pl.ds(al(slot * TOK, TOK), TOK), :]
        for k in range(1, 8):
            yy, cc = half(k)
            col = al((yy * 4 + h * 2 + cc) * ROWS, ROWS)
            sent.append(send(tok_h.at[0, :, pl.ds(col, ROWS)], dst, s_o.at[k - 1], v_o, dev(zl, x, yy, h, cc)))
        col = al(f * ROWS, ROWS)
        pltpu.make_async_copy(tok_h.at[0, :, pl.ds(col, ROWS)], dst, v_o).start()

    zb, zp = lax.rem(zl, 2), lax.div(zl, 2)
    near = dev(zl + 1 - 2 * zb, x, y, h, c)
    far = dev(zl + 2 - 4 * zp, x, y, h, c)
    owners = (3 - zb - 2 * zp, 1 - zb + 2 * zp, zb + 2 - 2 * zp, zl)

    def piece(k):
        return al(owners[k] * 32, 32)

    def send_r1(k):
        dst = lr.at[x, pl.ds(piece(k), 32), :]
        for d in (2, 1, 3):
            row = al(lax.rem(x + d, 4) * 128 + piece(k), 32)
            sent.append(send(local_h.at[0, pl.ds(row, 32), :], dst, s_r1.at[k, d - 1], v_r1.at[k], to_x(d)))
        row = al(x * 128 + piece(k), 32)
        pltpu.make_async_copy(local_h.at[0, pl.ds(row, 32), :], dst, v_r1.at[k]).start()

    send_c(0)
    for i in range(4):
        send_r1(i)
        send_a(i)
    for b in (1, 2, 3):
        send_c(b)
    send_o()

    load_pos.wait()
    pos = pos_v[0]

    def mask_slot(s, carry):
        first = (lax.rem(s, 4) * 4 + h * 2 + lax.div(s, 4)) * TOK
        place = first + lax.broadcasted_iota(jnp.int32, (TOK, 1), 0)
        hit = jnp.where(pos == place, 1.0, 0.0)
        any_hit = jnp.max(hit, axis=1, keepdims=True)
        mask_v[pl.ds(al(s * TOK, TOK), TOK), :] = jnp.broadcast_to(any_hit, (TOK, 128)).astype(BF)
        return carry

    lax.fori_loop(0, 8, mask_slot, 0)

    load_emb.wait()
    emb = emb_v[...].astype(F32)
    line = lax.broadcasted_iota(jnp.int32, (64, 128), 0)
    theirs = y * 4 + (1 - h) * 2 + c
    for a in range(NA):
        cols = slice(a * CA, (a + 1) * CA)
        ev[0:1, cols] = jnp.sum(jnp.where(line == theirs * NA + a, emb, 0.0), axis=0, keepdims=True)
        ev[1:2, cols] = jnp.sum(jnp.where(line == f * NA + a, emb, 0.0), axis=0, keepdims=True)

    load_base.wait()

    def dequant(k):
        await_bytes(lr.at[:, pl.ds(piece(k), 32), :], v_r1.at[k])
        row = al(x * 128 + piece(k), 32)
        if k == 2:
            await_bytes(r2r.at[0], v_r2.at[0])

        def block(i, carry):
            cols = pl.ds(al(i * QBLOCK, QBLOCK), QBLOCK)
            at = base_v[pl.ds(row, 32), cols]
            total = jnp.zeros((32, QBLOCK), F32)
            for s in range(4):
                drift = at - lr[s, pl.ds(piece(k), 32), cols].astype(F32)
                scale = (jnp.max(jnp.abs(drift), axis=1, keepdims=True) + 1e-6).astype(BF).astype(F32)
                code = (drift / scale).astype(BF).astype(F32)
                total = total + code * scale
            if k == 2:
                total = total + r2r[0, :, cols].astype(F32)
            if k < 3:
                r2s[k, :, cols] = total.astype(BF)
            else:
                own[:, cols] = total
            return carry

        lax.fori_loop(0, COLS // QBLOCK, block, 0)
        if k < 3:
            sent.append(send(r2s.at[k], r2r.at[k], s_r2.at[k], v_r2.at[k], near if k < 2 else far))

    def forward_c(b):
        mine = pl.ds(al(c * 512, 512), 512)
        await_bytes(cb.at[b, mine, :], v_c.at[b])
        sent.append(send(cb.at[b, mine, :], cb.at[b, mine, :], s_f.at[b], v_f.at[b], other_core))

    def have_c(b):
        theirs_ = pl.ds(al((1 - c) * 512, 512), 512)
        await_bytes(cb.at[b, theirs_, :], v_f.at[b])

    def take_a(a):
        await_bytes(xa.at[a], v_a.at[a])
        fill = jnp.broadcast_to(ev[0:1, a * CA:(a + 1) * CA].astype(BF), (HALF, CA))
        xa[a] = jnp.where(mask_v[...] > 0, fill, xa[a])

    def term(lhs, b):
        return lax.dot_general(lhs, cb[b], (((0,), (0,)), ((), ())), preferred_element_type=F32)

    def partial(a, b):
        ps[b, pl.ds(al(a * CA, CA), CA), :] = term(xa[a], b).astype(BF)

    forward_c(0)
    for a in range(NA):
        dequant(a)
        if a == 0:
            have_c(0)
        take_a(a)
        partial(a, 0)
        part = pl.ds(a * CA, CA)
        send(ps.at[0, part, :], pr.at[0, part, :], s_p.at[0, a], v_p.at[0, a], antipode)

    def column(b, first=0, last=NA):
        def one(a, carry):
            partial(a, b)
            rows = pl.ds(al(a * CA, CA), CA)
            send(ps.at[b, rows, :], pr.at[b, rows, :], s_p.at[b, a], v_p.at[b, a], antipode)
            return carry

        if first == 0:
            have_c(b)
        lax.fori_loop(first, last, one, 0)

    forward_c(1)
    column(1, 0, 2)
    for k in (1, 2):
        await_bytes(r2r.at[k], v_r2.at[k])
    mine = pl.ds(al(x * 128 + zl * 32, 32), 32)
    total = own[...]
    for k in (1, 2):
        total = total + r2r[k].astype(F32)
    og[mine, :] = (total * (1.0 / 16.0)).astype(BF)
    for k in (1, 2, 3):
        sent.append(send(og.at[mine, :], og.at[mine, :], s_r3.at[k - 1], v_r3.at[k - 1], to_z(k)))
    forward_c(2)
    forward_c(3)
    for k in (1, 2, 3):
        row = al(x * 128 + lax.rem(zl + 4 - k, 4) * 32, 32)
        await_bytes(og.at[pl.ds(row, 32), :], v_r3.at[k - 1])
    rows_x = pl.ds(al(x * 128, 128), 128)
    for k in (1, 2, 3):
        sent.append(send(og.at[rows_x, :], og.at[rows_x, :], s_r4.at[k - 1], v_r4.at[k - 1], to_x(k)))

    column(1, 2, NA)
    column(2)
    column(3)
    await_bytes(xo, v_o)

    def fill_o(s, carry):
        rows = pl.ds(al(s * TOK, TOK), TOK)
        m = mask_v[rows, :] > 0
        for a in range(NA):
            cols = slice(a * CA, (a + 1) * CA)
            fill = jnp.broadcast_to(ev[1:2, cols].astype(BF), (TOK, CA))
            xo[rows, cols] = jnp.where(m, fill, xo[rows, cols])
        return carry

    lax.fori_loop(0, 8, fill_o, 0)

    def own_term(b, carry):
        for a in range(NA):
            q[b, a * CA:(a + 1) * CA, :] = term(xo[:, a * CA:(a + 1) * CA], b)
        return carry

    lax.fori_loop(0, NB, own_term, 0)

    for k in (1, 2, 3):
        row = al(lax.rem(x + 4 - k, 4) * 128, 128)
        await_bytes(og.at[pl.ds(row, 128), :], v_r4.at[k - 1])
    load_mom.wait()

    def outer(i, carry):
        rows = pl.ds(al(i * 32, 32), 32)
        grad = og[rows, :].astype(F32)
        after = momentum_decay * mom_v[rows, :] + grad
        nm_v[rows, :] = after.astype(BF)
        base_v[rows, :] = base_v[rows, :] - outer_rate * (grad + momentum_decay * after)
        return carry

    lax.fori_loop(0, 16, outer, 0)

    for cp in sent:
        cp.wait_send()

    def finish(b, lo, n):
        rows = slice(lo, lo + n)
        cols = slice(b * CB, (b + 1) * CB)
        gradient = (q[b, rows, :] + pr[b, rows, :].astype(F32)) * D ** (-0.5)
        st_v[0, rows, cols] = (base_v[rows, cols] - inner_rate * gradient).astype(BF)

    for b in range(NB):
        for a in range(NA):
            part = pl.ds(a * CA, CA)
            await_bytes(pr.at[b, part, :], v_p.at[b, a])
            finish(b, a * CA, CA)
            await_bytes(ps.at[b, part, :], s_p.at[b, a])


def body(base, local, momentum, tokens, mask_embed, mask_pos, cotangent):
    hbm = pl.BlockSpec(memory_space=pltpu.HBM)
    dma = pltpu.SemaphoreType.DMA
    new_momentum, stepped = pl.pallas_call(
        kernel,
        name="step",
        out_shape=(
            pltpu.VMEM((ROWS, COLS), BF),
            pltpu.VMEM((1, ROWS, COLS), BF),
        ),
        in_specs=[hbm] * 7,
        out_specs=(pl.BlockSpec(memory_space=pltpu.VMEM),) * 2,
        scratch_shapes=[
            pltpu.VMEM((ROWS, COLS), F32),
            pltpu.VMEM((ROWS, COLS), F32),
            pltpu.VMEM((4, 128, COLS), BF),
            pltpu.VMEM((3, 32, COLS), BF),
            pltpu.VMEM((3, 32, COLS), BF),
            pltpu.VMEM((32, COLS), F32),
            pltpu.VMEM((ROWS, COLS), BF),
            pltpu.VMEM((NA, HALF, CA), BF),
            pltpu.VMEM((HALF, ROWS), BF),
            pltpu.VMEM((NB, HALF, CB), BF),
            pltpu.VMEM((HALF, 128), BF),
            pltpu.VMEM((8, ROWS), F32),
            pltpu.VMEM((NB, ROWS, CB), BF),
            pltpu.VMEM((NB, ROWS, CB), BF),
            pltpu.VMEM((NB, ROWS, CB), F32),
            pltpu.VMEM((1, 1, 768), jnp.int32),
            pltpu.VMEM((64, 128), BF),
            dma((NB, 3)),
            dma((NB,)),
            dma((NA, 7)),
            dma((7,)),
            dma((NB, NA)),
            dma((4, 3)),
            dma((3,)),
            dma((3,)),
            dma((3,)),
            dma((NB,)),
            dma((NB,)),
            dma((NA,)),
            dma(()),
            dma((NB, NA)),
            dma((4,)),
            dma((3,)),
            dma((3,)),
            dma((3,)),
            dma((4,)),
        ],
        compiler_params=pltpu.CompilerParams(
            collective_id=0, has_side_effects=True, vmem_limit_bytes=60 * 2**20
        ),
    )(base, local, momentum, tokens, mask_embed.reshape(64, 128), mask_pos, cotangent)
    return new_momentum, stepped


def solution(mesh):
    in_specs = (
        P("fsdp", None),
        P("replica", "fsdp", None),
        P("fsdp", None),
        P("replica", "fsdp", None),
        P(),
        P("replica", None, None),
        P("replica", "fsdp", None),
    )
    out_specs = (P("fsdp", None), P("replica", "fsdp", None))
    return jax.shard_map(body, mesh=mesh, in_specs=in_specs, out_specs=out_specs, check_vma=False)
```

```python
import jax
import jax.numpy as jnp
from jax import lax
from jax.experimental import pallas as pl
from jax.experimental.pallas import tpu as pltpu
from jax.sharding import PartitionSpec as P

D = 8192
ROWS = 512
COLS = 1024
TOK = 128
QBLOCK = 128
NB = 4
CB = COLS // NB
NA = 4
CA = ROWS // NA
HALF = 1024

momentum_decay = 0.9
outer_rate = 0.7
inner_rate = 0.5

MESH = pl.DeviceIdType.MESH
BF = jnp.bfloat16
F32 = jnp.float32


def al(v, m):
    return pl.multiple_of(v, m)


def kernel(base_h, local_h, mom_h, tok_h, emb_h, pos_h, cot_h, nm_v, st_v,
           base_v, mom_v, lr, r2s, r2r, own, og, xa, xo, cb, mask_v, ev, ps, pr, q, pos_v, emb_v,
           s_c, s_f, s_a, s_o, s_p, s_r1, s_r2, s_r3, s_r4,
           v_c, v_f, v_a, v_o, v_p, v_r1, v_r2, v_r3, v_r4, l_sem):
    r = lax.axis_index("replica")
    f = lax.axis_index("fsdp")
    zl, x = lax.div(r, 4), lax.rem(r, 4)
    y, h, c = lax.div(f, 4), lax.rem(lax.div(f, 2), 2), lax.rem(f, 2)
    slot = c * 4 + y

    def dev(zl_, x_, y_, h_, c_):
        return {"replica": zl_ * 4 + x_, "fsdp": y_ * 4 + h_ * 2 + c_}

    def half(k):
        t = lax.rem(slot + k, 8)
        return lax.rem(t, 4), lax.div(t, 4)

    def to_y(k):
        return dev(zl, x, lax.rem(y + k, 4), h, c)

    def to_x(k):
        return dev(zl, lax.rem(x + k, 4), y, h, c)

    def to_z(k):
        return dev(lax.rem(zl + k, 4), x, y, h, c)

    other_core = dev(zl, x, y, h, 1 - c)
    antipode = dev(zl, x, y, 1 - h, c)

    def send(src, dst, ss, rs, to):
        cp = pltpu.make_async_remote_copy(
            src_ref=src, dst_ref=dst, send_sem=ss, recv_sem=rs, device_id=to, device_id_type=MESH
        )
        cp.start()
        return cp

    def await_bytes(ref, sem):
        pltpu.make_async_copy(ref, ref, sem).wait()

    load_base = pltpu.make_async_copy(base_h, base_v, l_sem.at[0])
    load_mom = pltpu.make_async_copy(mom_h, mom_v, l_sem.at[1])
    load_pos = pltpu.make_async_copy(pos_h, pos_v, l_sem.at[2])
    load_pos.start()
    load_emb = pltpu.make_async_copy(emb_h, emb_v, l_sem.at[3])
    load_emb.start()
    load_base.start()
    load_mom.start()

    barrier = pltpu.get_barrier_semaphore()
    partners = [other_core, antipode]
    for k in (1, 2, 3):
        partners += [to_x(k), to_z(k)]
    for k in range(1, 8):
        yy, cc = half(k)
        partners.append(dev(zl, x, yy, h, cc))
    partners = partners[1:]
    for p in partners:
        pl.semaphore_signal(barrier, inc=1, device_id=p, device_id_type=MESH)
    pl.semaphore_wait(barrier, len(partners))

    sent = []

    def send_c(b):
        src = cot_h.at[0, :, pl.ds(b * CB, CB)]
        dst = cb.at[b, pl.ds(al(slot * TOK, TOK), TOK), :]
        for k in (2, 1, 3):
            sent.append(send(src, dst, s_c.at[b, k - 1], v_c.at[b], to_y(k)))
        pltpu.make_async_copy(src, dst, v_c.at[b]).start()

    def send_a(a):
        dst = xa.at[a, pl.ds(al(slot * TOK, TOK), TOK), :]
        for k in range(1, 8):
            yy, cc = half(k)
            col = al((yy * 4 + (1 - h) * 2 + cc) * ROWS + a * CA, CA)
            sent.append(send(tok_h.at[0, :, pl.ds(col, CA)], dst, s_a.at[a, k - 1], v_a.at[a], dev(zl, x, yy, h, cc)))
        col = al((y * 4 + (1 - h) * 2 + c) * ROWS + a * CA, CA)
        pltpu.make_async_copy(tok_h.at[0, :, pl.ds(col, CA)], dst, v_a.at[a]).start()

    def send_o():
        dst = xo.at[pl.ds(al(slot * TOK, TOK), TOK), :]
        for k in range(1, 8):
            yy, cc = half(k)
            col = al((yy * 4 + h * 2 + cc) * ROWS, ROWS)
            sent.append(send(tok_h.at[0, :, pl.ds(col, ROWS)], dst, s_o.at[k - 1], v_o, dev(zl, x, yy, h, cc)))
        col = al(f * ROWS, ROWS)
        pltpu.make_async_copy(tok_h.at[0, :, pl.ds(col, ROWS)], dst, v_o).start()

    zb, zp = lax.rem(zl, 2), lax.div(zl, 2)
    near = dev(zl + 1 - 2 * zb, x, y, h, c)
    far = dev(zl + 2 - 4 * zp, x, y, h, c)
    owners = (3 - zb - 2 * zp, 1 - zb + 2 * zp, zb + 2 - 2 * zp, zl)

    def piece(k):
        return al(owners[k] * 32, 32)

    def send_r1(k):
        dst = lr.at[x, pl.ds(piece(k), 32), :]
        for d in (2, 1, 3):
            row = al(lax.rem(x + d, 4) * 128 + piece(k), 32)
            sent.append(send(local_h.at[0, pl.ds(row, 32), :], dst, s_r1.at[k, d - 1], v_r1.at[k], to_x(d)))
        row = al(x * 128 + piece(k), 32)
        pltpu.make_async_copy(local_h.at[0, pl.ds(row, 32), :], dst, v_r1.at[k]).start()

    send_c(0)
    for i in range(4):
        send_r1(i)
        send_a(i)
    for b in (1, 2, 3):
        send_c(b)
    send_o()

    load_pos.wait()
    pos = pos_v[0]

    def mask_slot(s, carry):
        first = (lax.rem(s, 4) * 4 + h * 2 + lax.div(s, 4)) * TOK
        place = first + lax.broadcasted_iota(jnp.int32, (TOK, 1), 0)
        hit = jnp.where(pos == place, 1.0, 0.0)
        any_hit = jnp.max(hit, axis=1, keepdims=True)
        mask_v[pl.ds(al(s * TOK, TOK), TOK), :] = jnp.broadcast_to(any_hit, (TOK, 128)).astype(BF)
        return carry

    lax.fori_loop(0, 8, mask_slot, 0)

    load_emb.wait()
    emb = emb_v[...].astype(F32)
    line = lax.broadcasted_iota(jnp.int32, (64, 128), 0)
    theirs = y * 4 + (1 - h) * 2 + c
    for a in range(NA):
        cols = slice(a * CA, (a + 1) * CA)
        ev[0:1, cols] = jnp.sum(jnp.where(line == theirs * NA + a, emb, 0.0), axis=0, keepdims=True)
        ev[1:2, cols] = jnp.sum(jnp.where(line == f * NA + a, emb, 0.0), axis=0, keepdims=True)

    load_base.wait()

    def dequant(k):
        await_bytes(lr.at[:, pl.ds(piece(k), 32), :], v_r1.at[k])
        row = al(x * 128 + piece(k), 32)
        if k == 2:
            await_bytes(r2r.at[0], v_r2.at[0])

        def block(i, carry):
            cols = pl.ds(al(i * QBLOCK, QBLOCK), QBLOCK)
            at = base_v[pl.ds(row, 32), cols]
            total = jnp.zeros((32, QBLOCK), F32)
            for s in range(4):
                drift = at - lr[s, pl.ds(piece(k), 32), cols].astype(F32)
                scale = (jnp.max(jnp.abs(drift), axis=1, keepdims=True) + 1e-6).astype(BF).astype(F32)
                code = (drift / scale).astype(BF).astype(F32)
                total = total + code * scale
            if k == 2:
                total = total + r2r[0, :, cols].astype(F32)
            if k < 3:
                r2s[k, :, cols] = total.astype(BF)
            else:
                own[:, cols] = total
            return carry

        lax.fori_loop(0, COLS // QBLOCK, block, 0)
        if k < 3:
            sent.append(send(r2s.at[k], r2r.at[k], s_r2.at[k], v_r2.at[k], near if k < 2 else far))

    def forward_c(b):
        mine = pl.ds(al(c * 512, 512), 512)
        await_bytes(cb.at[b, mine, :], v_c.at[b])
        sent.append(send(cb.at[b, mine, :], cb.at[b, mine, :], s_f.at[b], v_f.at[b], other_core))

    def have_c(b):
        theirs_ = pl.ds(al((1 - c) * 512, 512), 512)
        await_bytes(cb.at[b, theirs_, :], v_f.at[b])

    def take_a(a):
        await_bytes(xa.at[a], v_a.at[a])
        fill = jnp.broadcast_to(ev[0:1, a * CA:(a + 1) * CA].astype(BF), (HALF, CA))
        xa[a] = jnp.where(mask_v[...] > 0, fill, xa[a])

    def term(lhs, b):
        return lax.dot_general(lhs, cb[b], (((0,), (0,)), ((), ())), preferred_element_type=F32)

    def partial(a, b):
        ps[b, pl.ds(al(a * CA, CA), CA), :] = term(xa[a], b).astype(BF)

    forward_c(0)
    for a in range(NA):
        dequant(a)
        if a == 0:
            have_c(0)
        take_a(a)
        partial(a, 0)
        part = pl.ds(a * CA, CA)
        send(ps.at[0, part, :], pr.at[0, part, :], s_p.at[0, a], v_p.at[0, a], antipode)

    def column(b, first=0, last=NA):
        def one(a, carry):
            partial(a, b)
            rows = pl.ds(al(a * CA, CA), CA)
            send(ps.at[b, rows, :], pr.at[b, rows, :], s_p.at[b, a], v_p.at[b, a], antipode)
            return carry

        if first == 0:
            have_c(b)
        lax.fori_loop(first, last, one, 0)

    forward_c(1)
    column(1, 0, 1)
    for k in (1, 2):
        await_bytes(r2r.at[k], v_r2.at[k])
    mine = pl.ds(al(x * 128 + zl * 32, 32), 32)
    total = own[...]
    for k in (1, 2):
        total = total + r2r[k].astype(F32)
    og[mine, :] = (total * (1.0 / 16.0)).astype(BF)
    for k in (1, 2, 3):
        sent.append(send(og.at[mine, :], og.at[mine, :], s_r3.at[k - 1], v_r3.at[k - 1], to_z(k)))
    forward_c(2)
    forward_c(3)
    for k in (1, 2, 3):
        row = al(x * 128 + lax.rem(zl + 4 - k, 4) * 32, 32)
        await_bytes(og.at[pl.ds(row, 32), :], v_r3.at[k - 1])
    rows_x = pl.ds(al(x * 128, 128), 128)
    for k in (1, 2, 3):
        sent.append(send(og.at[rows_x, :], og.at[rows_x, :], s_r4.at[k - 1], v_r4.at[k - 1], to_x(k)))

    column(1, 1, NA)
    column(2)
    column(3)
    await_bytes(xo, v_o)

    def fill_o(s, carry):
        rows = pl.ds(al(s * TOK, TOK), TOK)
        m = mask_v[rows, :] > 0
        for a in range(NA):
            cols = slice(a * CA, (a + 1) * CA)
            fill = jnp.broadcast_to(ev[1:2, cols].astype(BF), (TOK, CA))
            xo[rows, cols] = jnp.where(m, fill, xo[rows, cols])
        return carry

    lax.fori_loop(0, 8, fill_o, 0)

    def own_term(b, carry):
        for a in range(NA):
            q[b, a * CA:(a + 1) * CA, :] = term(xo[:, a * CA:(a + 1) * CA], b)
        return carry

    lax.fori_loop(0, NB, own_term, 0)

    for k in (1, 2, 3):
        row = al(lax.rem(x + 4 - k, 4) * 128, 128)
        await_bytes(og.at[pl.ds(row, 128), :], v_r4.at[k - 1])
    load_mom.wait()

    def outer(i, carry):
        rows = pl.ds(al(i * 32, 32), 32)
        grad = og[rows, :].astype(F32)
        after = momentum_decay * mom_v[rows, :] + grad
        nm_v[rows, :] = after.astype(BF)
        base_v[rows, :] = base_v[rows, :] - outer_rate * (grad + momentum_decay * after)
        return carry

    lax.fori_loop(0, 16, outer, 0)

    for cp in sent:
        cp.wait_send()

    def finish(b, lo, n):
        rows = slice(lo, lo + n)
        cols = slice(b * CB, (b + 1) * CB)
        gradient = (q[b, rows, :] + pr[b, rows, :].astype(F32)) * D ** (-0.5)
        st_v[0, rows, cols] = (base_v[rows, cols] - inner_rate * gradient).astype(BF)

    for b in range(NB):
        for a in range(NA):
            part = pl.ds(a * CA, CA)
            await_bytes(pr.at[b, part, :], v_p.at[b, a])
            finish(b, a * CA, CA)
            await_bytes(ps.at[b, part, :], s_p.at[b, a])


def body(base, local, momentum, tokens, mask_embed, mask_pos, cotangent):
    hbm = pl.BlockSpec(memory_space=pltpu.HBM)
    dma = pltpu.SemaphoreType.DMA
    new_momentum, stepped = pl.pallas_call(
        kernel,
        name="step",
        out_shape=(
            pltpu.VMEM((ROWS, COLS), BF),
            pltpu.VMEM((1, ROWS, COLS), BF),
        ),
        in_specs=[hbm] * 7,
        out_specs=(pl.BlockSpec(memory_space=pltpu.VMEM),) * 2,
        scratch_shapes=[
            pltpu.VMEM((ROWS, COLS), F32),
            pltpu.VMEM((ROWS, COLS), F32),
            pltpu.VMEM((4, 128, COLS), BF),
            pltpu.VMEM((3, 32, COLS), BF),
            pltpu.VMEM((3, 32, COLS), BF),
            pltpu.VMEM((32, COLS), F32),
            pltpu.VMEM((ROWS, COLS), BF),
            pltpu.VMEM((NA, HALF, CA), BF),
            pltpu.VMEM((HALF, ROWS), BF),
            pltpu.VMEM((NB, HALF, CB), BF),
            pltpu.VMEM((HALF, 128), BF),
            pltpu.VMEM((8, ROWS), F32),
            pltpu.VMEM((NB, ROWS, CB), BF),
            pltpu.VMEM((NB, ROWS, CB), BF),
            pltpu.VMEM((NB, ROWS, CB), F32),
            pltpu.VMEM((1, 1, 768), jnp.int32),
            pltpu.VMEM((64, 128), BF),
            dma((NB, 3)),
            dma((NB,)),
            dma((NA, 7)),
            dma((7,)),
            dma((NB, NA)),
            dma((4, 3)),
            dma((3,)),
            dma((3,)),
            dma((3,)),
            dma((NB,)),
            dma((NB,)),
            dma((NA,)),
            dma(()),
            dma((NB, NA)),
            dma((4,)),
            dma((3,)),
            dma((3,)),
            dma((3,)),
            dma((4,)),
        ],
        compiler_params=pltpu.CompilerParams(
            collective_id=0, has_side_effects=True, vmem_limit_bytes=60 * 2**20
        ),
    )(base, local, momentum, tokens, mask_embed.reshape(64, 128), mask_pos, cotangent)
    return new_momentum, stepped


def solution(mesh):
    in_specs = (
        P("fsdp", None),
        P("replica", "fsdp", None),
        P("fsdp", None),
        P("replica", "fsdp", None),
        P(),
        P("replica", None, None),
        P("replica", "fsdp", None),
    )
    out_specs = (P("fsdp", None), P("replica", "fsdp", None))
    return jax.shard_map(body, mesh=mesh, in_specs=in_specs, out_specs=out_specs, check_vma=False)
```

```python
import jax
import jax.numpy as jnp
from jax import lax
from jax.experimental import pallas as pl
from jax.experimental.pallas import tpu as pltpu
from jax.sharding import PartitionSpec as P

D = 8192
ROWS = 512
COLS = 1024
TOK = 128
QBLOCK = 128
NB = 4
CB = COLS // NB
NA = 4
CA = ROWS // NA
HALF = 1024

momentum_decay = 0.9
outer_rate = 0.7
inner_rate = 0.5

MESH = pl.DeviceIdType.MESH
BF = jnp.bfloat16
F32 = jnp.float32


def al(v, m):
    return pl.multiple_of(v, m)


def kernel(base_h, local_h, mom_h, tok_h, emb_h, pos_h, cot_h, nm_v, st_v,
           base_v, mom_v, lr, r2s, r2r, own, og, xa, xo, cb, mask_v, ev, ps, pr, q, pos_v, emb_v,
           s_c, s_f, s_a, s_o, s_p, s_r1, s_r2, s_r3, s_r4,
           v_c, v_f, v_a, v_o, v_p, v_r1, v_r2, v_r3, v_r4, l_sem):
    r = lax.axis_index("replica")
    f = lax.axis_index("fsdp")
    zl, x = lax.div(r, 4), lax.rem(r, 4)
    y, h, c = lax.div(f, 4), lax.rem(lax.div(f, 2), 2), lax.rem(f, 2)
    slot = c * 4 + y

    def dev(zl_, x_, y_, h_, c_):
        return {"replica": zl_ * 4 + x_, "fsdp": y_ * 4 + h_ * 2 + c_}

    def half(k):
        t = lax.rem(slot + k, 8)
        return lax.rem(t, 4), lax.div(t, 4)

    def to_y(k):
        return dev(zl, x, lax.rem(y + k, 4), h, c)

    def to_x(k):
        return dev(zl, lax.rem(x + k, 4), y, h, c)

    def to_z(k):
        return dev(lax.rem(zl + k, 4), x, y, h, c)

    other_core = dev(zl, x, y, h, 1 - c)
    antipode = dev(zl, x, y, 1 - h, c)

    def send(src, dst, ss, rs, to):
        cp = pltpu.make_async_remote_copy(
            src_ref=src, dst_ref=dst, send_sem=ss, recv_sem=rs, device_id=to, device_id_type=MESH
        )
        cp.start()
        return cp

    def await_bytes(ref, sem):
        pltpu.make_async_copy(ref, ref, sem).wait()

    load_base = pltpu.make_async_copy(base_h, base_v, l_sem.at[0])
    load_mom = pltpu.make_async_copy(mom_h, mom_v, l_sem.at[1])
    load_pos = pltpu.make_async_copy(pos_h, pos_v, l_sem.at[2])
    load_pos.start()
    load_emb = pltpu.make_async_copy(emb_h, emb_v, l_sem.at[3])
    load_emb.start()
    load_base.start()
    load_mom.start()

    barrier = pltpu.get_barrier_semaphore()
    partners = [other_core, antipode]
    for k in (1, 2, 3):
        partners += [to_x(k), to_z(k)]
    for k in range(1, 8):
        yy, cc = half(k)
        partners.append(dev(zl, x, yy, h, cc))
    partners = partners[1:]
    for p in partners:
        pl.semaphore_signal(barrier, inc=1, device_id=p, device_id_type=MESH)
    pl.semaphore_wait(barrier, len(partners))

    sent = []

    def send_c(b):
        src = cot_h.at[0, :, pl.ds(b * CB, CB)]
        dst = cb.at[b, pl.ds(al(slot * TOK, TOK), TOK), :]
        for k in (2, 1, 3):
            sent.append(send(src, dst, s_c.at[b, k - 1], v_c.at[b], to_y(k)))
        pltpu.make_async_copy(src, dst, v_c.at[b]).start()

    def send_a(a):
        dst = xa.at[a, pl.ds(al(slot * TOK, TOK), TOK), :]
        for k in range(1, 8):
            yy, cc = half(k)
            col = al((yy * 4 + (1 - h) * 2 + cc) * ROWS + a * CA, CA)
            sent.append(send(tok_h.at[0, :, pl.ds(col, CA)], dst, s_a.at[a, k - 1], v_a.at[a], dev(zl, x, yy, h, cc)))
        col = al((y * 4 + (1 - h) * 2 + c) * ROWS + a * CA, CA)
        pltpu.make_async_copy(tok_h.at[0, :, pl.ds(col, CA)], dst, v_a.at[a]).start()

    def send_o():
        dst = xo.at[pl.ds(al(slot * TOK, TOK), TOK), :]
        for k in range(1, 8):
            yy, cc = half(k)
            col = al((yy * 4 + h * 2 + cc) * ROWS, ROWS)
            sent.append(send(tok_h.at[0, :, pl.ds(col, ROWS)], dst, s_o.at[k - 1], v_o, dev(zl, x, yy, h, cc)))
        col = al(f * ROWS, ROWS)
        pltpu.make_async_copy(tok_h.at[0, :, pl.ds(col, ROWS)], dst, v_o).start()

    zb, zp = lax.rem(zl, 2), lax.div(zl, 2)
    near = dev(zl + 1 - 2 * zb, x, y, h, c)
    far = dev(zl + 2 - 4 * zp, x, y, h, c)
    owners = (3 - zb - 2 * zp, 1 - zb + 2 * zp, zb + 2 - 2 * zp, zl)

    def piece(k):
        return al(owners[k] * 32, 32)

    def send_r1(k):
        dst = lr.at[x, pl.ds(piece(k), 32), :]
        for d in (2, 1, 3):
            row = al(lax.rem(x + d, 4) * 128 + piece(k), 32)
            sent.append(send(local_h.at[0, pl.ds(row, 32), :], dst, s_r1.at[k, d - 1], v_r1.at[k], to_x(d)))
        row = al(x * 128 + piece(k), 32)
        pltpu.make_async_copy(local_h.at[0, pl.ds(row, 32), :], dst, v_r1.at[k]).start()

    send_c(0)
    for i in range(4):
        send_a(i)
        send_r1(i)
    for b in (1, 2, 3):
        send_c(b)
    send_o()

    load_pos.wait()
    pos = pos_v[0]

    def mask_slot(s, carry):
        first = (lax.rem(s, 4) * 4 + h * 2 + lax.div(s, 4)) * TOK
        place = first + lax.broadcasted_iota(jnp.int32, (TOK, 1), 0)
        hit = jnp.where(pos == place, 1.0, 0.0)
        any_hit = jnp.max(hit, axis=1, keepdims=True)
        mask_v[pl.ds(al(s * TOK, TOK), TOK), :] = jnp.broadcast_to(any_hit, (TOK, 128)).astype(BF)
        return carry

    lax.fori_loop(0, 8, mask_slot, 0)

    load_emb.wait()
    emb = emb_v[...].astype(F32)
    line = lax.broadcasted_iota(jnp.int32, (64, 128), 0)
    theirs = y * 4 + (1 - h) * 2 + c
    for a in range(NA):
        cols = slice(a * CA, (a + 1) * CA)
        ev[0:1, cols] = jnp.sum(jnp.where(line == theirs * NA + a, emb, 0.0), axis=0, keepdims=True)
        ev[1:2, cols] = jnp.sum(jnp.where(line == f * NA + a, emb, 0.0), axis=0, keepdims=True)

    load_base.wait()

    def dequant(k):
        await_bytes(lr.at[:, pl.ds(piece(k), 32), :], v_r1.at[k])
        row = al(x * 128 + piece(k), 32)
        if k == 2:
            await_bytes(r2r.at[0], v_r2.at[0])

        def block(i, carry):
            cols = pl.ds(al(i * QBLOCK, QBLOCK), QBLOCK)
            at = base_v[pl.ds(row, 32), cols]
            total = jnp.zeros((32, QBLOCK), F32)
            for s in range(4):
                drift = at - lr[s, pl.ds(piece(k), 32), cols].astype(F32)
                scale = (jnp.max(jnp.abs(drift), axis=1, keepdims=True) + 1e-6).astype(BF).astype(F32)
                code = (drift / scale).astype(BF).astype(F32)
                total = total + code * scale
            if k == 2:
                total = total + r2r[0, :, cols].astype(F32)
            if k < 3:
                r2s[k, :, cols] = total.astype(BF)
            else:
                own[:, cols] = total
            return carry

        lax.fori_loop(0, COLS // QBLOCK, block, 0)
        if k < 3:
            sent.append(send(r2s.at[k], r2r.at[k], s_r2.at[k], v_r2.at[k], near if k < 2 else far))

    def forward_c(b):
        mine = pl.ds(al(c * 512, 512), 512)
        await_bytes(cb.at[b, mine, :], v_c.at[b])
        sent.append(send(cb.at[b, mine, :], cb.at[b, mine, :], s_f.at[b], v_f.at[b], other_core))

    def have_c(b):
        theirs_ = pl.ds(al((1 - c) * 512, 512), 512)
        await_bytes(cb.at[b, theirs_, :], v_f.at[b])

    def take_a(a):
        await_bytes(xa.at[a], v_a.at[a])
        fill = jnp.broadcast_to(ev[0:1, a * CA:(a + 1) * CA].astype(BF), (HALF, CA))
        xa[a] = jnp.where(mask_v[...] > 0, fill, xa[a])

    def term(lhs, b):
        return lax.dot_general(lhs, cb[b], (((0,), (0,)), ((), ())), preferred_element_type=F32)

    def partial(a, b):
        ps[b, pl.ds(al(a * CA, CA), CA), :] = term(xa[a], b).astype(BF)

    forward_c(0)
    for a in range(NA):
        dequant(a)
        if a == 0:
            have_c(0)
        take_a(a)
        partial(a, 0)
        part = pl.ds(a * CA, CA)
        send(ps.at[0, part, :], pr.at[0, part, :], s_p.at[0, a], v_p.at[0, a], antipode)

    def column(b, first=0, last=NA):
        def one(a, carry):
            partial(a, b)
            rows = pl.ds(al(a * CA, CA), CA)
            send(ps.at[b, rows, :], pr.at[b, rows, :], s_p.at[b, a], v_p.at[b, a], antipode)
            return carry

        if first == 0:
            have_c(b)
        lax.fori_loop(first, last, one, 0)

    forward_c(1)
    column(1, 0, 1)
    for k in (1, 2):
        await_bytes(r2r.at[k], v_r2.at[k])
    mine = pl.ds(al(x * 128 + zl * 32, 32), 32)
    total = own[...]
    for k in (1, 2):
        total = total + r2r[k].astype(F32)
    og[mine, :] = (total * (1.0 / 16.0)).astype(BF)
    for k in (1, 2, 3):
        sent.append(send(og.at[mine, :], og.at[mine, :], s_r3.at[k - 1], v_r3.at[k - 1], to_z(k)))
    forward_c(2)
    forward_c(3)
    for k in (1, 2, 3):
        row = al(x * 128 + lax.rem(zl + 4 - k, 4) * 32, 32)
        await_bytes(og.at[pl.ds(row, 32), :], v_r3.at[k - 1])
    rows_x = pl.ds(al(x * 128, 128), 128)
    for k in (1, 2, 3):
        sent.append(send(og.at[rows_x, :], og.at[rows_x, :], s_r4.at[k - 1], v_r4.at[k - 1], to_x(k)))

    column(1, 1, NA)
    column(2)
    column(3)
    await_bytes(xo, v_o)

    def fill_o(s, carry):
        rows = pl.ds(al(s * TOK, TOK), TOK)
        m = mask_v[rows, :] > 0
        for a in range(NA):
            cols = slice(a * CA, (a + 1) * CA)
            fill = jnp.broadcast_to(ev[1:2, cols].astype(BF), (TOK, CA))
            xo[rows, cols] = jnp.where(m, fill, xo[rows, cols])
        return carry

    lax.fori_loop(0, 8, fill_o, 0)

    def own_term(b, carry):
        for a in range(NA):
            q[b, a * CA:(a + 1) * CA, :] = term(xo[:, a * CA:(a + 1) * CA], b)
        return carry

    lax.fori_loop(0, NB, own_term, 0)

    for k in (1, 2, 3):
        row = al(lax.rem(x + 4 - k, 4) * 128, 128)
        await_bytes(og.at[pl.ds(row, 128), :], v_r4.at[k - 1])
    load_mom.wait()

    def outer(i, carry):
        rows = pl.ds(al(i * 32, 32), 32)
        grad = og[rows, :].astype(F32)
        after = momentum_decay * mom_v[rows, :] + grad
        nm_v[rows, :] = after.astype(BF)
        base_v[rows, :] = base_v[rows, :] - outer_rate * (grad + momentum_decay * after)
        return carry

    lax.fori_loop(0, 16, outer, 0)

    for cp in sent:
        cp.wait_send()

    def finish(b, lo, n):
        rows = slice(lo, lo + n)
        cols = slice(b * CB, (b + 1) * CB)
        gradient = (q[b, rows, :] + pr[b, rows, :].astype(F32)) * D ** (-0.5)
        st_v[0, rows, cols] = (base_v[rows, cols] - inner_rate * gradient).astype(BF)

    for b in range(NB):
        for a in range(NA):
            part = pl.ds(a * CA, CA)
            await_bytes(pr.at[b, part, :], v_p.at[b, a])
            finish(b, a * CA, CA)
            await_bytes(ps.at[b, part, :], s_p.at[b, a])


def body(base, local, momentum, tokens, mask_embed, mask_pos, cotangent):
    hbm = pl.BlockSpec(memory_space=pltpu.HBM)
    dma = pltpu.SemaphoreType.DMA
    new_momentum, stepped = pl.pallas_call(
        kernel,
        name="step",
        out_shape=(
            pltpu.VMEM((ROWS, COLS), BF),
            pltpu.VMEM((1, ROWS, COLS), BF),
        ),
        in_specs=[hbm] * 7,
        out_specs=(pl.BlockSpec(memory_space=pltpu.VMEM),) * 2,
        scratch_shapes=[
            pltpu.VMEM((ROWS, COLS), F32),
            pltpu.VMEM((ROWS, COLS), F32),
            pltpu.VMEM((4, 128, COLS), BF),
            pltpu.VMEM((3, 32, COLS), BF),
            pltpu.VMEM((3, 32, COLS), BF),
            pltpu.VMEM((32, COLS), F32),
            pltpu.VMEM((ROWS, COLS), BF),
            pltpu.VMEM((NA, HALF, CA), BF),
            pltpu.VMEM((HALF, ROWS), BF),
            pltpu.VMEM((NB, HALF, CB), BF),
            pltpu.VMEM((HALF, 128), BF),
            pltpu.VMEM((8, ROWS), F32),
            pltpu.VMEM((NB, ROWS, CB), BF),
            pltpu.VMEM((NB, ROWS, CB), BF),
            pltpu.VMEM((NB, ROWS, CB), F32),
            pltpu.VMEM((1, 1, 768), jnp.int32),
            pltpu.VMEM((64, 128), BF),
            dma((NB, 3)),
            dma((NB,)),
            dma((NA, 7)),
            dma((7,)),
            dma((NB, NA)),
            dma((4, 3)),
            dma((3,)),
            dma((3,)),
            dma((3,)),
            dma((NB,)),
            dma((NB,)),
            dma((NA,)),
            dma(()),
            dma((NB, NA)),
            dma((4,)),
            dma((3,)),
            dma((3,)),
            dma((3,)),
            dma((4,)),
        ],
        compiler_params=pltpu.CompilerParams(
            collective_id=0, has_side_effects=True, vmem_limit_bytes=60 * 2**20
        ),
    )(base, local, momentum, tokens, mask_embed.reshape(64, 128), mask_pos, cotangent)
    return new_momentum, stepped


def solution(mesh):
    in_specs = (
        P("fsdp", None),
        P("replica", "fsdp", None),
        P("fsdp", None),
        P("replica", "fsdp", None),
        P(),
        P("replica", None, None),
        P("replica", "fsdp", None),
    )
    out_specs = (P("fsdp", None), P("replica", "fsdp", None))
    return jax.shard_map(body, mesh=mesh, in_specs=in_specs, out_specs=out_specs, check_vma=False)
```
